1024 devices in a mesh: ctx: 32 (over y_lo, x, core), fsdp: 32 (over y_hi, z).
Axes of the slice: x: 4, y: 8 (y_hi: 2, y_lo: 4; y = y_hi * 4 + y_lo), z: 16, core: 2. Of those that a mesh axis runs over, the one named last changes fastest.
Arguments:
- queries: bfloat16 [32, 4096, 768], P('fsdp', 'ctx'), may hold values from -6 to 6
- key_rows: bfloat16 [32, 4096, 768], P('fsdp', 'ctx'), may hold values from -6 to 6
- value_rows: bfloat16 [32, 4096, 768], P('fsdp', 'ctx'), may hold values from -6 to 6
- lengths: int32 [32], P('fsdp'), may hold values from 2048 to 4096, as said below
- out_weight: bfloat16 [768, 1536], P(None, 'fsdp'), may hold values from -0.21875 to 0.21875
Outputs:
- mixed: bfloat16 [32, 4096, 1536], P('fsdp', 'ctx')
The draws below stay inside these ranges and needn't reach their ends.
Inputs may be any that keep to these rules, and one draw needn't show every extreme that they name: `lengths`: keys at frame positions at or beyond a recording's length are ignored.
All inputs are finite; a program needn't handle non-finite values.
Results may differ from the reference program's by a relative error of at most 0.011.
Values may be sent and summed in bfloat16 or wider, within the bound.
A program may use at most 128 MiB of HBM per device.

```python
import math
import jax
import jax.numpy as jnp
from jax import lax

D = 1536
HEADS = 8
HDIM = 96
HD = 768
FRAMES = 4096
RECS = 32


def draw_queries(key, part):
    base_key = jax.random.fold_in(key, 1)
    values = jnp.clip(1.6 * jax.random.normal(base_key, (RECS, FRAMES, HEADS * HDIM), jnp.float32), -6.0, 6.0)
    return values.astype(jnp.bfloat16)


def draw_key_rows(key, part):
    base_key = jax.random.fold_in(key, 2)
    values = jnp.clip(1.6 * jax.random.normal(base_key, (RECS, FRAMES, HEADS * HDIM), jnp.float32), -6.0, 6.0)
    return values.astype(jnp.bfloat16)


def draw_lengths(key, part):
    key_base, key_order = jax.random.split(jax.random.fold_in(key, 3))
    drawn = jax.random.randint(key_base, (RECS,), FRAMES // 2, FRAMES + 1)
    order = jax.random.permutation(key_order, RECS)
    drawn = drawn.at[order[0]].set(FRAMES)
    drawn = drawn.at[order[1]].set(FRAMES // 2)
    return drawn.astype(jnp.int32)


def levels(key, extent, shards, least, top_value):
    gain, own = 1.0, jax.random.fold_in(key, 6)
    for axis_at, blocks in shards:
        heights = jnp.exp(jax.random.uniform(jax.random.fold_in(own, axis_at), (blocks,), jnp.float32, least / len(shards), top_value / len(shards)))
        gain = gain * jnp.repeat(heights, extent[axis_at] // blocks).reshape([-1 if axis == axis_at else 1 for axis in range(len(extent))])
    return gain


def centred(own_key, extent, scale, most, cuts=(), kind=jnp.bfloat16):
    values = scale * jax.random.normal(own_key, extent, jnp.float32)
    if cuts:
        values = values * levels(own_key, extent, cuts, -0.22, 0.18)
    return jnp.clip(values, -most, most).astype(kind)


def setup_inputs(seed: int = 0) -> dict:
    keys = jax.random.split(jax.random.key(seed), 6)
    return {
        "queries": draw_queries(jax.random.fold_in(keys[5], 71), 0),
        "key_rows": draw_key_rows(jax.random.fold_in(keys[5], 71), 0),
        "value_rows": centred(keys[2], (RECS, FRAMES, HD), 1.0, 6.0, ((0, 32), (1, 32))),
        "lengths": draw_lengths(jax.random.fold_in(keys[5], 71), 0),
        "out_weight": centred(keys[4], (HD, D), HD ** -0.5, 0.21875, ((1, 32),)),
    }


def reference(queries, key_rows, value_rows, lengths, out_weight):
    frames = queries.shape[1]
    feature_width = queries.shape[2]
    head_size = feature_width // HEADS
    score_scale = 1.0 / math.sqrt(head_size)

    def per_recording(items):
        query_one, key_one, value_one, valid_frames = items
        inside = jnp.arange(frames, dtype=jnp.int32) < valid_frames
        outputs = []
        for head in range(HEADS):
            columns = slice(head * head_size, (head + 1) * head_size)
            scores = jnp.dot(query_one[:, columns], key_one[:, columns].T, preferred_element_type=jnp.float32) * score_scale
            scores = jnp.where(inside[None, :], scores, jnp.float32(-1e+30))
            row_max = lax.optimization_barrier(jnp.max(scores, axis=-1, keepdims=True))
            probs = jnp.where(inside[None, :], jnp.exp(scores - row_max), jnp.float32(0.0))
            row_sum = lax.optimization_barrier(jnp.sum(probs, axis=-1, keepdims=True))
            head_out = jnp.dot(probs.astype(jnp.bfloat16), value_one[:, columns], preferred_element_type=jnp.float32) / row_sum
            outputs.append(head_out)
        attention = jnp.concatenate(outputs, axis=1).astype(jnp.bfloat16)
        return jnp.dot(attention, out_weight, preferred_element_type=jnp.float32).astype(jnp.bfloat16)
    return lax.map(per_recording, (queries, key_rows, value_rows, lengths))
```

```python
import functools
import math

import jax
import jax.numpy as jnp
from jax import lax
from jax.experimental import pallas as pl
from jax.experimental.pallas import tpu as pltpu
from jax.sharding import PartitionSpec as P

HEADS = 8
LANES = 128
NY, NX, NC, NZ = 4, 4, 2, 16
STAGES = ((0, 2), (2, 3), (3, 5), (5, 6))
QROWS = 256
MESH = pl.DeviceIdType.MESH
NEG = -1e30


def head_tiles(head, size):
    return range(head * size // LANES, (head * size + size - 1) // LANES + 1)


def kernel(
    len_ref, q_hbm, k_hbm, v_hbm, w_hbm, out_ref,
    qbuf, kv, osend, orecv, sstat, ssend, srecv, wbuf,
    loc, kvs, kvr, qup, qdn, qr, osem, orsem, ssem, srsem,
    wrs, wrr, wls, wlr, wbs, wbr, wps, wpr,
):
    ntile = qbuf.shape[0]
    rows = qbuf.shape[2]
    size = ntile * LANES // HEADS
    nkeys = NX * NC * rows
    ctx = lax.axis_index("ctx")
    fs = lax.axis_index("fsdp")
    c = lax.rem(ctx, NC)
    x = lax.rem(lax.div(ctx, NC), NX)
    y = lax.div(ctx, NC * NX)
    hi = lax.div(fs, NZ)
    z = lax.rem(fs, NZ)

    def at_y(row):
        return {"ctx": row * (NX * NC) + x * NC + c}

    def at_x(col):
        return {"ctx": y * (NX * NC) + col * NC + c}

    def at_z(plane):
        return {"fsdp": hi * NZ + plane}

    sib = {"ctx": y * (NX * NC) + x * NC + (1 - c)}
    xr, xl = lax.rem(x + 1, NX), lax.rem(x + NX - 1, NX)
    xo = lax.rem(x + 2, NX)
    zr, zl = lax.rem(z + 1, NZ), lax.rem(z + NZ - 1, NZ)
    partner = {"fsdp": (1 - hi) * NZ + z}

    def remote(src, dst, send, recv, device):
        return pltpu.make_async_remote_copy(
            src_ref=src, dst_ref=dst, send_sem=send, recv_sem=recv, device_id=device, device_id_type=MESH
        )

    def own_copies(t):
        cols = pl.ds(t * LANES, LANES)
        s = x * NC + c
        return (
            pltpu.make_async_copy(k_hbm.at[:, cols], kv.at[0, t, s], loc.at[0, t]),
            pltpu.make_async_copy(v_hbm.at[:, cols], kv.at[1, t, s], loc.at[1, t]),
            pltpu.make_async_copy(q_hbm.at[:, cols], qbuf.at[t, y], loc.at[2, t]),
        )

    wbase = c * NZ

    for t in range(ntile):
        for copy in own_copies(t):
            copy.start()

    barrier = pltpu.get_barrier_semaphore()
    peers = [at_y(lax.rem(y + d, NY)) for d in range(1, NY)]
    peers += [at_x(xr), at_x(xl), sib, at_z(zr), at_z(zl), partner]
    for peer in peers:
        pl.semaphore_signal(barrier, inc=1, device_id=peer, device_id_type=MESH)
    pl.semaphore_wait(barrier, len(peers))

    def kv_at(which, stage, col, core):
        lo, hi_t = STAGES[stage]
        s = col * NC + core
        if which is None:
            return kv.at[:, lo:hi_t, s]
        return kv.at[which, lo:hi_t, s]

    kv_moves = (
        (None, x, xl, at_x(xr), c),
        (None, x, xr, at_x(xl), c),
        (None, x, x, sib, 1 - c),
        (0, xl, xo, at_x(xr), c),
        (1, xr, xo, at_x(xl), c),
        (None, xl, xl, sib, 1 - c),
        (None, xr, xr, sib, 1 - c),
        (0, xo, xo, sib, 1 - c),
        (1, xo, xo, sib, 1 - c),
    )

    def kv_send(stage, i):
        what, col, _, device, _ = kv_moves[i]
        ref = kv_at(what, stage, col, c)
        return remote(ref, ref, kvs.at[stage, i], kvr.at[stage, i], device)

    def kv_recv(stage, i):
        what, _, col, device, core = kv_moves[i]
        ref = kv_at(what, stage, col, core)
        return remote(ref, ref, kvs.at[stage, i], kvr.at[stage, i], device)

    def q_move(stage, row, up):
        lo, hi_t = STAGES[stage]
        ref = qbuf.at[lo:hi_t, row]
        send = qup if up else qdn
        return remote(ref, ref, send.at[stage, row], qr.at[stage, row], at_y(y + 1 if up else y - 1))

    def q_both(stage, row, op):
        @pl.when(y < NY - 1)
        def _():
            op(q_move(stage, row, True))

        @pl.when(y > 0)
        def _():
            op(q_move(stage, row, False))

    def q_forward(stage, d):
        @pl.when(y >= d)
        def _():
            q_move(stage, y - d, True).wait_recv()

            @pl.when(y < NY - 1)
            def _():
                q_move(stage, y - d, True).start()

        @pl.when(y + d < NY)
        def _():
            q_move(stage, y + d, False).wait_recv()

            @pl.when(y > 0)
            def _():
                q_move(stage, y + d, False).start()

    def q_drain(stage):
        q_both(stage, y, lambda copy: copy.wait_send())
        for d in range(1, NY):

            @pl.when((y >= d) & (y < NY - 1))
            def _():
                q_move(stage, y - d, True).wait_send()

            @pl.when((y + d < NY) & (y > 0))
            def _():
                q_move(stage, y + d, False).wait_send()

    def w_at(plane):
        return wbuf.at[wbase + plane]

    def w_ring(step, right, recv):
        sems = (wrs, wrr) if right else (wls, wlr)
        if right:
            plane = lax.rem(z + NZ - (step if recv else step - 1), NZ)
        else:
            plane = lax.rem(z + (step if recv else step - 1), NZ)
        ref = w_at(plane)
        return remote(ref, ref, sems[0].at[step - 1], sems[1].at[step - 1], at_z(zr if right else zl))

    def w_share(k, plane):
        ref = w_at(plane)
        return remote(ref, ref, wbs.at[k], wbr.at[k], sib)

    def w_shared(k, plane):
        ref = wbuf.at[(1 - c) * NZ + plane]
        return remote(ref, ref, wbs.at[k], wbr.at[k], sib)

    def w_partner():
        ref = w_at(z)
        return remote(ref, ref, wps.at[0], wpr.at[0], partner)

    nright, nleft = NZ // 2, NZ // 2 - 1

    def w_step(step):
        if step <= nright:
            w_ring(step, True, True).wait_recv()
            if step < nright:
                w_ring(step + 1, True, False).start()
            w_share(step, lax.rem(z + NZ - step, NZ)).start()
        if step <= nleft:
            w_ring(step, False, True).wait_recv()
            if step < nleft:
                w_ring(step + 1, False, False).start()
            w_share(nright + step, lax.rem(z + step, NZ)).start()

    for stage, (lo, hi_t) in enumerate(STAGES):
        for t in range(lo, hi_t):
            for copy in own_copies(t):
                copy.wait()
        q_both(stage, y, lambda copy: copy.start())
        for i in range(3):
            kv_send(stage, i).start()

    @pl.when(c == hi)
    def _():
        own_w = pltpu.make_async_copy(w_hbm, w_at(z), loc.at[0, 0])
        own_w.start()
        own_w.wait()
        w_partner().start()

    @pl.when(c != hi)
    def _():
        w_partner().wait_recv()

    w_ring(1, True, False).start()
    w_ring(1, False, False).start()
    w_share(0, z).start()

    def near(stage):
        kv_recv(stage, 0).wait_recv()
        kv_send(stage, 3).start()
        kv_send(stage, 5).start()
        kv_recv(stage, 1).wait_recv()
        kv_send(stage, 4).start()
        kv_send(stage, 6).start()
        q_forward(stage, 1)

    def far(stage):
        q_forward(stage, 2)
        q_forward(stage, 3)
        kv_recv(stage, 3).wait_recv()
        kv_send(stage, 7).start()
        kv_recv(stage, 4).wait_recv()
        kv_send(stage, 8).start()

    def here(stage):
        for i in (2, 5, 6, 7, 8):
            kv_recv(stage, i).wait_recv()

    scale = math.log2(math.e) / math.sqrt(size)
    key_at = lax.broadcasted_iota(jnp.int32, (1, nkeys), 1) + y * nkeys
    bias = jnp.where(key_at < len_ref[0], jnp.float32(0.0), jnp.float32(NEG))
    chunks = QROWS // rows

    def attend(head):
        tiles = head_tiles(head, size)
        width = len(tiles) * LANES
        first = head * size - tiles[0] * LANES
        lane = lax.broadcasted_iota(jnp.int32, (1, width), 1)
        mine = jnp.where((lane >= first) & (lane < first + size), 1.0, 0.0).astype(jnp.bfloat16)
        lane1 = lax.broadcasted_iota(jnp.int32, (1, LANES), 1)

        def window(pick, count):
            return jnp.concatenate([pick(t).reshape(count, LANES) for t in tiles], axis=1)

        def body(i, carry):
            span = pl.ds(i * chunks, chunks)
            qw = window(lambda t: qbuf[t, span], QROWS) * mine
            kw = window(lambda t: kv[0, t], nkeys)
            s = lax.dot_general(qw, kw, (((1,), (1,)), ((), ())), preferred_element_type=jnp.float32)
            s = s * scale + bias
            m = jnp.max(s, axis=-1, keepdims=True)
            p = jnp.exp2(s - m)
            total = jnp.sum(p, axis=-1, keepdims=True)
            vw = window(lambda t: kv[1, t], nkeys)
            o = jnp.dot(p.astype(jnp.bfloat16), vw, preferred_element_type=jnp.float32)
            o = o / total
            lse = m + jnp.log2(total)
            for n, t in enumerate(tiles):
                part = o[:, n * LANES : (n + 1) * LANES].reshape(chunks, rows, LANES)
                start = head * size - t * LANES
                if start > 0:
                    old = osend[t, span].astype(jnp.float32)
                    part = jnp.where(lane1[None] >= start, part, old)
                osend[t, span] = part.astype(jnp.bfloat16)
            stat = lse.reshape(chunks, rows, 1)
            old = sstat[span] if head else jnp.float32(0.0)
            sstat[span] = jnp.where(lane1[None] == head, stat, old)
            return carry

        lax.fori_loop(0, NY // chunks, body, 0)

    def o_move(t, d):
        dest = lax.rem(y + d, NY)
        return remote(osend.at[t, dest], orecv.at[t, d - 1], osem.at[t, d - 1], orsem.at[t, d - 1], at_y(dest))

    def s_move(d):
        dest = lax.rem(y + d, NY)
        return remote(ssend.at[dest], srecv.at[d - 1], ssem.at[d - 1], srsem.at[d - 1], at_y(dest))

    near(0)
    near(1)
    far(0)
    nstage = len(STAGES)
    per = HEADS // nstage
    for stage in range(nstage):
        here(stage)
        for n in range(per):
            head = stage * per + n
            attend(head)
            if n == 0:
                if stage + 2 < nstage:
                    near(stage + 2)
                if stage + 1 < nstage:
                    far(stage + 1)
            w_step(head + 1)
            for t in head_tiles(head, size):
                if (t * LANES + LANES - 1) // size == head:
                    for d in range(1, NY):
                        o_move(t, d).start()

    for j in range(NY):
        ssend[j] = sstat[j].T[:HEADS]
    for d in range(1, NY):
        s_move(d).start()
    for d in range(1, NY):
        s_move(d).wait_recv()

    lses = [ssend[y]] + [srecv[d - 1] for d in range(1, NY)]
    top = functools.reduce(jnp.maximum, lses)
    parts = [jnp.exp2(lse - top) for lse in lses]
    whole = functools.reduce(jnp.add, parts)
    weights = jnp.concatenate(
        [part / whole for part in parts] + [jnp.zeros((LANES - NY * HEADS, rows), jnp.float32)], axis=0
    ).T
    lane1 = lax.broadcasted_iota(jnp.int32, (1, LANES), 1)
    merged = []
    for t in range(ntile):
        first, last = t * LANES // size, (t * LANES + LANES - 1) // size
        cut = last * size - t * LANES
        total = None
        for j in range(NY):
            if j:
                o_move(t, j).wait_recv()
                value = orecv[t, j - 1]
            else:
                value = osend[t, y]
            a = weights[:, j * HEADS + first : j * HEADS + first + 1]
            b = weights[:, j * HEADS + last : j * HEADS + last + 1]
            term = jnp.where(lane1 < cut, a, b) * value.astype(jnp.float32)
            total = term if total is None else total + term
        merged.append(total.astype(jnp.bfloat16))
    attention = jnp.concatenate(merged, axis=1)

    w_shared(0, z).wait_recv()
    for step in range(1, nright + 1):
        w_shared(step, lax.rem(z + NZ - step, NZ)).wait_recv()
    for step in range(1, nleft + 1):
        w_shared(nright + step, lax.rem(z + step, NZ)).wait_recv()

    half = wbuf.shape[0] // 2
    ncols = half * wbuf.shape[1]
    for n in range(2):
        wn = wbuf[n * half : (n + 1) * half].reshape(ncols, ntile * LANES)
        out_ref[:, n * ncols : (n + 1) * ncols] = lax.dot_general(
            attention, wn, (((1,), (1,)), ((), ())), preferred_element_type=jnp.float32
        ).astype(jnp.bfloat16)

    for stage in range(nstage):
        q_drain(stage)
        for i in range(len(kv_moves)):
            kv_send(stage, i).wait_send()
    for t in range(ntile):
        for d in range(1, NY):
            o_move(t, d).wait_send()
    for d in range(1, NY):
        s_move(d).wait_send()

    @pl.when(c == hi)
    def _():
        w_partner().wait_send()

    for step in range(1, nright + 1):
        w_ring(step, True, False).wait_send()
        w_share(step, z).wait_send()
    for step in range(1, nleft + 1):
        w_ring(step, False, False).wait_send()
        w_share(nright + step, z).wait_send()
    w_share(0, z).wait_send()


def per_device(queries, key_rows, value_rows, lengths, out_weight):
    rows, feats = queries.shape[1:]
    ntile = feats // LANES
    columns = out_weight.shape[1]
    nstage = len(STAGES)
    dma = pltpu.SemaphoreType.DMA
    anywhere = pl.BlockSpec(memory_space=pl.ANY)
    mixed = pl.pallas_call(
        kernel,
        out_shape=jax.ShapeDtypeStruct((rows, columns * 2 * NZ), jnp.bfloat16),
        in_specs=[pl.BlockSpec(memory_space=pltpu.SMEM)] + [anywhere] * 4,
        out_specs=pl.BlockSpec(memory_space=pltpu.VMEM),
        scratch_shapes=[
            pltpu.VMEM((ntile, NY, rows, LANES), jnp.bfloat16),
            pltpu.VMEM((2, ntile, NX * NC, rows, LANES), jnp.bfloat16),
            pltpu.VMEM((ntile, NY, rows, LANES), jnp.bfloat16),
            pltpu.VMEM((ntile, NY - 1, rows, LANES), jnp.bfloat16),
            pltpu.VMEM((NY, rows, LANES), jnp.float32),
            pltpu.VMEM((NY, HEADS, rows), jnp.float32),
            pltpu.VMEM((NY - 1, HEADS, rows), jnp.float32),
            pltpu.VMEM((2 * NZ, columns, feats), jnp.bfloat16),
            dma((3, ntile)),
            dma((nstage, 9)),
            dma((nstage, 9)),
            dma((nstage, NY)),
            dma((nstage, NY)),
            dma((nstage, NY)),
            dma((ntile, NY - 1)),
            dma((ntile, NY - 1)),
            dma((NY - 1,)),
            dma((NY - 1,)),
            dma((NZ // 2,)),
            dma((NZ // 2,)),
            dma((NZ // 2,)),
            dma((NZ // 2,)),
            dma((NZ,)),
            dma((NZ,)),
            dma((1,)),
            dma((1,)),
        ],
        compiler_params=pltpu.CompilerParams(
            collective_id=0, has_side_effects=True, vmem_limit_bytes=48 * 1024 * 1024
        ),
        name="attention",
    )(lengths, queries[0], key_rows[0], value_rows[0], out_weight.T)
    return mixed[None]


def solution(mesh):
    return jax.shard_map(
        per_device,
        mesh=mesh,
        in_specs=(
            P("fsdp", "ctx", None),
            P("fsdp", "ctx", None),
            P("fsdp", "ctx", None),
            P("fsdp"),
            P(None, "fsdp"),
        ),
        out_specs=P("fsdp", "ctx", None),
        check_vma=False,
    )
```

```python
import functools
import math

import jax
import jax.numpy as jnp
from jax import lax
from jax.experimental import pallas as pl
from jax.experimental.pallas import tpu as pltpu
from jax.sharding import PartitionSpec as P

HEADS = 8
LANES = 128
NY, NX, NC, NZ = 4, 4, 2, 16
STAGES = tuple((t, t + 1) for t in range(6))
STAGE_HEADS = ((0,), (1,), (2, 3), (4,), (5,), (6, 7))
QROWS = 512
AHEAD = 2
W_AFTER = (1, 4, 6)
MESH = pl.DeviceIdType.MESH
NEG = -1e30


def head_tiles(head, size):
    return range(head * size // LANES, (head * size + size - 1) // LANES + 1)


def kernel(
    len_ref, q_hbm, k_hbm, v_hbm, w_hbm, out_ref,
    qbuf, kv, osend, orecv, sstat, ssend, srecv, wbuf,
    loc, kvs, kvr, qs, qr, osem, orsem, ssem, srsem,
    wrs, wrr, wls, wlr, wbs, wbr, wps, wpr,
):
    ntile = qbuf.shape[0]
    rows = qbuf.shape[2]
    size = ntile * LANES // HEADS
    nkeys = NX * NC * rows
    ctx = lax.axis_index("ctx")
    fs = lax.axis_index("fsdp")
    c = lax.rem(ctx, NC)
    x = lax.rem(lax.div(ctx, NC), NX)
    y = lax.div(ctx, NC * NX)
    hi = lax.div(fs, NZ)
    z = lax.rem(fs, NZ)

    def at_y(row):
        return {"ctx": row * (NX * NC) + x * NC + c}

    def at_x(col):
        return {"ctx": y * (NX * NC) + col * NC + c}

    def at_z(plane):
        return {"fsdp": hi * NZ + plane}

    sib = {"ctx": y * (NX * NC) + x * NC + (1 - c)}
    xr, xl = lax.rem(x + 1, NX), lax.rem(x + NX - 1, NX)
    xo = lax.rem(x + 2, NX)

    def z_at(offset):
        return lax.rem(z + offset + NZ, NZ)

    partner = {"fsdp": (1 - hi) * NZ + z}

    def remote(src, dst, send, recv, device):
        return pltpu.make_async_remote_copy(
            src_ref=src, dst_ref=dst, send_sem=send, recv_sem=recv, device_id=device, device_id_type=MESH
        )

    def own_copy(which, t):
        source = (k_hbm, v_hbm, q_hbm)[which].at[:, pl.ds(t * LANES, LANES)]
        target = qbuf.at[t, y] if which == 2 else kv.at[which, t, x * NC + c]
        return pltpu.make_async_copy(source, target, loc.at[which, t])

    wbase = c * NZ

    def own_w():
        return pltpu.make_async_copy(w_hbm, wbuf.at[wbase + z], loc.at[3, 0])

    @pl.when(c == hi)
    def _():
        own_w().start()

    for t in range(ntile):
        for which in range(3):
            own_copy(which, t).start()

    barrier = pltpu.get_barrier_semaphore()
    peers = [at_y(lax.rem(y + d, NY)) for d in range(1, NY)]
    peers += [at_x(xr), at_x(xl), sib, partner]
    peers += [at_z(z_at(offset)) for offset in (-2, -1, 1, 2)]
    for peer in peers:
        pl.semaphore_signal(barrier, inc=1, device_id=peer, device_id_type=MESH)
    pl.semaphore_wait(barrier, len(peers))

    def kv_at(which, stage, col, core):
        lo, hi_t = STAGES[stage]
        s = col * NC + core
        if which is None:
            return kv.at[:, lo:hi_t, s]
        return kv.at[which, lo:hi_t, s]

    kv_moves = (
        (None, x, xl, at_x(xr), c),
        (None, x, xr, at_x(xl), c),
        (None, x, x, sib, 1 - c),
        (0, xl, xo, at_x(xr), c),
        (1, xr, xo, at_x(xl), c),
        (None, xl, xl, sib, 1 - c),
        (None, xr, xr, sib, 1 - c),
        (0, xo, xo, sib, 1 - c),
        (1, xo, xo, sib, 1 - c),
    )

    def kv_send(stage, i):
        what, col, _, device, _ = kv_moves[i]
        ref = kv_at(what, stage, col, c)
        return remote(ref, ref, kvs.at[stage, i], kvr.at[stage, i], device)

    def kv_recv(stage, i):
        what, _, col, device, core = kv_moves[i]
        ref = kv_at(what, stage, col, core)
        return remote(ref, ref, kvs.at[stage, i], kvr.at[stage, i], device)

    pair = y + 1 - 2 * lax.rem(y, 2)
    upper = lax.div(y, 2)
    far_rows = (2 - upper, 3 - 3 * upper)
    outward = 1 - lax.rem(lax.div(y + 1, 2), 2)
    inner, outer = outward == 0, outward == 1

    def q_move(stage, kind):
        lo, hi_t = STAGES[stage]
        row = y if kind < 2 else far_rows[kind - 2]
        ref = qbuf.at[lo:hi_t, row]
        slot = (0, 1 + outward, 1, 2)[kind]
        device = at_y(far_rows[0] if kind == 1 else pair)
        return remote(ref, ref, qs.at[stage, kind], qr.at[stage, slot], device)

    def q_recv(stage, slot):
        lo, hi_t = STAGES[stage]
        ref = qbuf.at[lo:hi_t, (pair, *far_rows)[slot]]
        return remote(ref, ref, qs.at[stage, 0], qr.at[stage, slot], at_y(pair))

    def w_at(plane):
        return wbuf.at[wbase + plane]

    def w_ring(dist, right, recv):
        sems = (wrs, wrr) if right else (wls, wlr)
        sign = -1 if right else 1
        hop = 2 - dist % 2
        ref = w_at(z_at(sign * (dist if recv else dist - hop)))
        device = at_z(z_at(-sign * hop))
        return remote(ref, ref, sems[0].at[dist - 1], sems[1].at[dist - 1], device)

    def w_share(k, plane):
        ref = w_at(plane)
        return remote(ref, ref, wbs.at[k], wbr.at[k], sib)

    def w_shared(k, plane):
        ref = wbuf.at[(1 - c) * NZ + plane]
        return remote(ref, ref, wbs.at[k], wbr.at[k], sib)

    def w_partner():
        ref = w_at(z)
        return remote(ref, ref, wps.at[0], wpr.at[0], partner)

    nright, nleft = NZ // 2, NZ // 2 - 1

    def w_step(step):
        for right, most in ((True, nright), (False, nleft)):
            base = 0 if right else nright
            sign = -1 if right else 1
            for dist in (2 * step, 2 * step - 1):
                if dist > most:
                    continue
                w_ring(dist, right, True).wait_recv()
                if dist == 2 * step:
                    for later in range(dist + 1, min(dist + 2, most) + 1):
                        w_ring(later, right, False).start()
                w_share(base + dist, z_at(sign * dist)).start()

    def own_q(stage):
        for t in range(*STAGES[stage]):
            own_copy(2, t).wait()
        for kind in range(2):
            q_move(stage, kind).start()

    def own(stage):
        for t in range(*STAGES[stage]):
            for which in range(2):
                own_copy(which, t).wait()
        for i in range(3):
            kv_send(stage, i).start()

    def w_first():
        @pl.when(c == hi)
        def _():
            own_w().wait()
            w_partner().start()

    def w_start():
        @pl.when(c != hi)
        def _():
            w_partner().wait_recv()

        for dist in (1, 2):
            w_ring(dist, True, False).start()
            w_ring(dist, False, False).start()
        w_share(0, z).start()

    def near(stage):
        for i in range(2):
            kv_recv(stage, i).wait_recv()
            kv_send(stage, i + 3).start()
            kv_send(stage, i + 5).start()

        @pl.when(inner)
        def _():
            for kind in range(2, 4):
                q_recv(stage, kind - 1).wait_recv()
                q_move(stage, kind).start()

    def far(stage):
        for i in range(3, 5):
            kv_recv(stage, i).wait_recv()
            kv_send(stage, i + 4).start()

    def here(stage):
        q_recv(stage, 0).wait_recv()

        @pl.when(outer)
        def _():
            for slot in range(1, 3):
                q_recv(stage, slot).wait_recv()

        for i in (2, 5, 6, 7, 8):
            kv_recv(stage, i).wait_recv()

    scale = math.log2(math.e) / math.sqrt(size)
    key_at = lax.broadcasted_iota(jnp.int32, (1, nkeys), 1) + y * nkeys
    bias = jnp.where(key_at < len_ref[0], jnp.float32(0.0), jnp.float32(NEG))
    chunks = QROWS // rows

    def attend(head):
        tiles = head_tiles(head, size)
        width = len(tiles) * LANES
        first = head * size - tiles[0] * LANES
        lane = lax.broadcasted_iota(jnp.int32, (1, width), 1)
        mine = jnp.where((lane >= first) & (lane < first + size), 1.0, 0.0).astype(jnp.bfloat16)
        lane1 = lax.broadcasted_iota(jnp.int32, (1, LANES), 1)

        def window(pick, count):
            return jnp.concatenate([pick(t).reshape(count, LANES) for t in tiles], axis=1)

        def body(i, carry):
            span = pl.ds(i * chunks, chunks)
            qw = window(lambda t: qbuf[t, span], QROWS) * mine
            kw = window(lambda t: kv[0, t], nkeys)
            s = lax.dot_general(qw, kw, (((1,), (1,)), ((), ())), preferred_element_type=jnp.float32)
            s = s * scale + bias
            m = jnp.max(s, axis=-1, keepdims=True)
            p = jnp.exp2(s - m)
            total = jnp.sum(p, axis=-1, keepdims=True)
            vw = window(lambda t: kv[1, t], nkeys)
            o = jnp.dot(p.astype(jnp.bfloat16), vw, preferred_element_type=jnp.float32)
            o = o / total
            lse = m + jnp.log2(total)
            for n, t in enumerate(tiles):
                part = o[:, n * LANES : (n + 1) * LANES].reshape(chunks, rows, LANES)
                start = head * size - t * LANES
                if start > 0:
                    old = osend[t, span].astype(jnp.float32)
                    part = jnp.where(lane1[None] >= start, part, old)
                osend[t, span] = part.astype(jnp.bfloat16)
            return lse

        lse = body(0, None)
        stat = sstat[...] if head else jnp.zeros((rows, LANES), jnp.float32)
        for j in range(NY):
            stat = jnp.where(lane1 == j * HEADS + head, lse[j * rows : (j + 1) * rows], stat)
        sstat[...] = stat
        return stat

    def o_move(t, d):
        dest = lax.rem(y + d, NY)
        return remote(osend.at[t, dest], orecv.at[t, d - 1], osem.at[t, d - 1], orsem.at[t, d - 1], at_y(dest))

    def s_move(d):
        dest = lax.rem(y + d, NY)
        return remote(ssend.at[dest], srecv.at[d - 1], ssem.at[d - 1], srsem.at[d - 1], at_y(dest))

    def head_and_send(head):
        stat = attend(head)
        for t in head_tiles(head, size):
            if (t * LANES + LANES - 1) // size == head:
                for d in range(1, NY):
                    o_move(t, d).start()
        if head == HEADS - 1:
            ssend[...] = stat.T[: NY * HEADS].reshape(NY, HEADS, rows)
            for d in range(1, NY):
                s_move(d).start()

    nstage = len(STAGES)
    w_first()
    for stage in range(AHEAD):
        own_q(stage)
        own(stage)
    for stage in range(AHEAD, nstage):
        own_q(stage)
    w_start()
    near(0)
    own(AHEAD)
    for stage, heads in enumerate(STAGE_HEADS):
        if stage + 1 < nstage:
            near(stage + 1)
        if stage + 1 + AHEAD < nstage:
            own(stage + 1 + AHEAD)
        far(stage)
        here(stage)
        for head in heads:
            head_and_send(head)
            if head in W_AFTER:
                w_step(W_AFTER.index(head) + 1)

    for d in range(1, NY):
        s_move(d).wait_recv()

    lses = [ssend[y]] + [srecv[d - 1] for d in range(1, NY)]
    top = functools.reduce(jnp.maximum, lses)
    parts = [jnp.exp2(lse - top) for lse in lses]
    whole = functools.reduce(jnp.add, parts)
    weights = jnp.concatenate(
        [part / whole for part in parts] + [jnp.zeros((LANES - NY * HEADS, rows), jnp.float32)], axis=0
    ).T
    lane1 = lax.broadcasted_iota(jnp.int32, (1, LANES), 1)
    merged = []
    for t in range(ntile):
        first, last = t * LANES // size, (t * LANES + LANES - 1) // size
        cut = last * size - t * LANES
        total = None
        for j in range(NY):
            if j:
                o_move(t, j).wait_recv()
                value = orecv[t, j - 1]
            else:
                value = osend[t, y]
            a = weights[:, j * HEADS + first : j * HEADS + first + 1]
            b = weights[:, j * HEADS + last : j * HEADS + last + 1]
            term = jnp.where(lane1 < cut, a, b) * value.astype(jnp.float32)
            total = term if total is None else total + term
        merged.append(total.astype(jnp.bfloat16))
    attention = jnp.concatenate(merged, axis=1)

    w_step(4)
    w_shared(0, z).wait_recv()
    for step in range(1, nright + 1):
        w_shared(step, lax.rem(z + NZ - step, NZ)).wait_recv()
    for step in range(1, nleft + 1):
        w_shared(nright + step, lax.rem(z + step, NZ)).wait_recv()

    half = wbuf.shape[0] // 2
    ncols = half * wbuf.shape[1]
    for n in range(2):
        wn = wbuf[n * half : (n + 1) * half].reshape(ncols, ntile * LANES)
        out_ref[:, n * ncols : (n + 1) * ncols] = lax.dot_general(
            attention, wn, (((1,), (1,)), ((), ())), preferred_element_type=jnp.float32
        ).astype(jnp.bfloat16)

    for stage in range(nstage):
        for kind in range(2):
            q_move(stage, kind).wait_send()

        @pl.when(inner)
        def _():
            for kind in range(2, 4):
                q_move(stage, kind).wait_send()

        for i in range(len(kv_moves)):
            kv_send(stage, i).wait_send()
    for t in range(ntile):
        for d in range(1, NY):
            o_move(t, d).wait_send()
    for d in range(1, NY):
        s_move(d).wait_send()

    @pl.when(c == hi)
    def _():
        w_partner().wait_send()

    for step in range(1, nright + 1):
        w_ring(step, True, False).wait_send()
        w_share(step, z).wait_send()
    for step in range(1, nleft + 1):
        w_ring(step, False, False).wait_send()
        w_share(nright + step, z).wait_send()
    w_share(0, z).wait_send()


def per_device(queries, key_rows, value_rows, lengths, out_weight):
    rows, feats = queries.shape[1:]
    ntile = feats // LANES
    columns = out_weight.shape[1]
    nstage = len(STAGES)
    dma = pltpu.SemaphoreType.DMA
    anywhere = pl.BlockSpec(memory_space=pltpu.HBM)
    mixed = pl.pallas_call(
        kernel,
        out_shape=jax.ShapeDtypeStruct((rows, columns * 2 * NZ), jnp.bfloat16),
        in_specs=[pl.BlockSpec(memory_space=pltpu.SMEM)] + [anywhere] * 4,
        out_specs=pl.BlockSpec(memory_space=pltpu.VMEM),
        scratch_shapes=[
            pltpu.VMEM((ntile, NY, rows, LANES), jnp.bfloat16),
            pltpu.VMEM((2, ntile, NX * NC, rows, LANES), jnp.bfloat16),
            pltpu.VMEM((ntile, NY, rows, LANES), jnp.bfloat16),
            pltpu.VMEM((ntile, NY - 1, rows, LANES), jnp.bfloat16),
            pltpu.VMEM((rows, LANES), jnp.float32),
            pltpu.VMEM((NY, HEADS, rows), jnp.float32),
            pltpu.VMEM((NY - 1, HEADS, rows), jnp.float32),
            pltpu.VMEM((2 * NZ, columns, feats), jnp.bfloat16),
            dma((4, ntile)),
            dma((nstage, 9)),
            dma((nstage, 9)),
            dma((nstage, 4)),
            dma((nstage, 3)),
            dma((ntile, NY - 1)),
            dma((ntile, NY - 1)),
            dma((NY - 1,)),
            dma((NY - 1,)),
            dma((NZ // 2,)),
            dma((NZ // 2,)),
            dma((NZ // 2,)),
            dma((NZ // 2,)),
            dma((NZ,)),
            dma((NZ,)),
            dma((1,)),
            dma((1,)),
        ],
        compiler_params=pltpu.CompilerParams(
            collective_id=0, has_side_effects=True, vmem_limit_bytes=63 * 1024 * 1024
        ),
        name="attention",
    )(lengths, queries[0], key_rows[0], value_rows[0], out_weight.T)
    return mixed[None]


def solution(mesh):
    return jax.shard_map(
        per_device,
        mesh=mesh,
        in_specs=(
            P("fsdp", "ctx", None),
            P("fsdp", "ctx", None),
            P("fsdp", "ctx", None),
            P("fsdp"),
            P(None, "fsdp"),
        ),
        out_specs=P("fsdp", "ctx", None),
        check_vma=False,
    )
```

```python
import functools
import math

import jax
import jax.numpy as jnp
from jax import lax
from jax.experimental import pallas as pl
from jax.experimental.pallas import tpu as pltpu
from jax.sharding import PartitionSpec as P

HEADS = 8
LANES = 128
NY, NX, NC, NZ = 4, 4, 2, 16
STAGES = tuple((t, t + 1) for t in range(6))
QROWS = 512
AHEAD = 2
ORDER = (
    "near0 own2 near1 own3",
    "far0 here0 head0",
    "near2 own4 far1",
    "here1 head1 w1",
    "near3 own5 far2",
    "here2 head2 near4 far3",
    "head3 here3 head4 w2",
    "near5 far4 here4 head5",
    "far5 here5 head6 w3",
    "head7",
)
MESH = pl.DeviceIdType.MESH
NEG = -1e30


def head_tiles(head, size):
    return range(head * size // LANES, (head * size + size - 1) // LANES + 1)


def kernel(
    len_ref, q_hbm, k_hbm, v_hbm, w_hbm, out_ref,
    qbuf, kv, osend, orecv, sstat, ssend, srecv, wbuf,
    loc, kvs, kvr, qs, qr, osem, orsem, ssem, srsem,
    wrs, wrr, wls, wlr, wbs, wbr, wps, wpr,
):
    ntile = qbuf.shape[0]
    rows = qbuf.shape[2]
    size = ntile * LANES // HEADS
    nkeys = NX * NC * rows
    ctx = lax.axis_index("ctx")
    fs = lax.axis_index("fsdp")
    c = lax.rem(ctx, NC)
    x = lax.rem(lax.div(ctx, NC), NX)
    y = lax.div(ctx, NC * NX)
    hi = lax.div(fs, NZ)
    z = lax.rem(fs, NZ)

    def at_y(row):
        return {"ctx": row * (NX * NC) + x * NC + c}

    def at_x(col):
        return {"ctx": y * (NX * NC) + col * NC + c}

    def at_z(plane):
        return {"fsdp": hi * NZ + plane}

    sib = {"ctx": y * (NX * NC) + x * NC + (1 - c)}
    xr, xl = lax.rem(x + 1, NX), lax.rem(x + NX - 1, NX)
    xo = lax.rem(x + 2, NX)

    def z_at(offset):
        return lax.rem(z + offset + NZ, NZ)

    partner = {"fsdp": (1 - hi) * NZ + z}

    def remote(src, dst, send, recv, device):
        return pltpu.make_async_remote_copy(
            src_ref=src, dst_ref=dst, send_sem=send, recv_sem=recv, device_id=device, device_id_type=MESH
        )

    def own_copy(which, t):
        source = (k_hbm, v_hbm, q_hbm)[which].at[:, pl.ds(t * LANES, LANES)]
        target = qbuf.at[t, y] if which == 2 else kv.at[which, t, x * NC + c]
        return pltpu.make_async_copy(source, target, loc.at[which, t])

    wbase = c * NZ

    def own_w():
        return pltpu.make_async_copy(w_hbm, wbuf.at[wbase + z], loc.at[3, 0])

    @pl.when(c == hi)
    def _():
        own_w().start()

    for t in range(ntile):
        for which in range(3):
            own_copy(which, t).start()

    barrier = pltpu.get_barrier_semaphore()
    peers = [at_y(lax.rem(y + d, NY)) for d in range(1, NY)]
    peers += [at_x(xr), at_x(xl), sib, partner]
    peers += [at_z(z_at(offset)) for offset in (-2, -1, 1, 2)]
    for peer in peers:
        pl.semaphore_signal(barrier, inc=1, device_id=peer, device_id_type=MESH)
    pl.semaphore_wait(barrier, len(peers))

    def kv_at(which, stage, col, core):
        lo, hi_t = STAGES[stage]
        s = col * NC + core
        if which is None:
            return kv.at[:, lo:hi_t, s]
        return kv.at[which, lo:hi_t, s]

    kv_moves = (
        (None, x, xl, at_x(xr), c),
        (None, x, xr, at_x(xl), c),
        (None, x, x, sib, 1 - c),
        (0, xl, xo, at_x(xr), c),
        (1, xr, xo, at_x(xl), c),
        (None, xl, xl, sib, 1 - c),
        (None, xr, xr, sib, 1 - c),
        (0, xo, xo, sib, 1 - c),
        (1, xo, xo, sib, 1 - c),
    )

    def kv_send(stage, i):
        what, col, _, device, _ = kv_moves[i]
        ref = kv_at(what, stage, col, c)
        return remote(ref, ref, kvs.at[stage, i], kvr.at[stage, i], device)

    def kv_recv(stage, i):
        what, _, col, device, core = kv_moves[i]
        ref = kv_at(what, stage, col, core)
        return remote(ref, ref, kvs.at[stage, i], kvr.at[stage, i], device)

    pair = y + 1 - 2 * lax.rem(y, 2)
    upper = lax.div(y, 2)
    far_rows = (2 - upper, 3 - 3 * upper)
    outward = 1 - lax.rem(lax.div(y + 1, 2), 2)
    inner, outer = outward == 0, outward == 1

    def q_move(stage, kind):
        lo, hi_t = STAGES[stage]
        row = y if kind < 2 else far_rows[kind - 2]
        ref = qbuf.at[lo:hi_t, row]
        slot = (0, 1 + outward, 1, 2)[kind]
        device = at_y(far_rows[0] if kind == 1 else pair)
        return remote(ref, ref, qs.at[stage, kind], qr.at[stage, slot], device)

    def q_recv(stage, slot):
        lo, hi_t = STAGES[stage]
        ref = qbuf.at[lo:hi_t, (pair, *far_rows)[slot]]
        return remote(ref, ref, qs.at[stage, 0], qr.at[stage, slot], at_y(pair))

    def w_at(plane):
        return wbuf.at[wbase + plane]

    def w_ring(dist, right, recv):
        sems = (wrs, wrr) if right else (wls, wlr)
        sign = -1 if right else 1
        hop = 2 - dist % 2
        ref = w_at(z_at(sign * (dist if recv else dist - hop)))
        device = at_z(z_at(-sign * hop))
        return remote(ref, ref, sems[0].at[dist - 1], sems[1].at[dist - 1], device)

    def w_share(k, plane):
        ref = w_at(plane)
        return remote(ref, ref, wbs.at[k], wbr.at[k], sib)

    def w_shared(k, plane):
        ref = wbuf.at[(1 - c) * NZ + plane]
        return remote(ref, ref, wbs.at[k], wbr.at[k], sib)

    def w_partner():
        ref = w_at(z)
        return remote(ref, ref, wps.at[0], wpr.at[0], partner)

    nright, nleft = NZ // 2, NZ // 2 - 1

    def w_step(step):
        for right, most in ((True, nright), (False, nleft)):
            base = 0 if right else nright
            sign = -1 if right else 1
            for dist in (2 * step, 2 * step - 1):
                if dist > most:
                    continue
                w_ring(dist, right, True).wait_recv()
                if dist == 2 * step:
                    for later in range(dist + 1, min(dist + 2, most) + 1):
                        w_ring(later, right, False).start()
                w_share(base + dist, z_at(sign * dist)).start()

    def own_q(stage):
        for t in range(*STAGES[stage]):
            own_copy(2, t).wait()
        for kind in range(2):
            q_move(stage, kind).start()

    def own(stage):
        for t in range(*STAGES[stage]):
            for which in range(2):
                own_copy(which, t).wait()
        for i in range(3):
            kv_send(stage, i).start()

    def w_first():
        @pl.when(c == hi)
        def _():
            own_w().wait()
            w_partner().start()

    def w_start():
        @pl.when(c != hi)
        def _():
            w_partner().wait_recv()

        for dist in (1, 2):
            w_ring(dist, True, False).start()
            w_ring(dist, False, False).start()
        w_share(0, z).start()

    def near(stage):
        for i in range(2):
            kv_recv(stage, i).wait_recv()
            kv_send(stage, i + 3).start()
            kv_send(stage, i + 5).start()

        @pl.when(inner)
        def _():
            for kind in range(2, 4):
                q_recv(stage, kind - 1).wait_recv()
                q_move(stage, kind).start()

    def far(stage):
        for i in range(3, 5):
            kv_recv(stage, i).wait_recv()
            kv_send(stage, i + 4).start()

    def here(stage):
        q_recv(stage, 0).wait_recv()

        @pl.when(outer)
        def _():
            for slot in range(1, 3):
                q_recv(stage, slot).wait_recv()

        for i in (2, 5, 6, 7, 8):
            kv_recv(stage, i).wait_recv()

    scale = math.log2(math.e) / math.sqrt(size)
    key_at = lax.broadcasted_iota(jnp.int32, (1, nkeys), 1) + y * nkeys
    bias = jnp.where(key_at < len_ref[0], jnp.float32(0.0), jnp.float32(NEG))
    chunks = QROWS // rows

    def attend(head):
        tiles = head_tiles(head, size)
        width = len(tiles) * LANES
        first = head * size - tiles[0] * LANES
        lane = lax.broadcasted_iota(jnp.int32, (1, width), 1)
        mine = jnp.where((lane >= first) & (lane < first + size), 1.0, 0.0).astype(jnp.bfloat16)
        lane1 = lax.broadcasted_iota(jnp.int32, (1, LANES), 1)

        def window(pick, count):
            return jnp.concatenate([pick(t).reshape(count, LANES) for t in tiles], axis=1)

        def body(i, carry):
            span = pl.ds(i * chunks, chunks)
            qw = window(lambda t: qbuf[t, span], QROWS) * mine
            kw = window(lambda t: kv[0, t], nkeys)
            s = lax.dot_general(qw, kw, (((1,), (1,)), ((), ())), preferred_element_type=jnp.float32)
            s = s * scale + bias
            m = jnp.max(s, axis=-1, keepdims=True)
            p = jnp.exp2(s - m)
            total = jnp.sum(p, axis=-1, keepdims=True)
            vw = window(lambda t: kv[1, t], nkeys)
            o = jnp.dot(p.astype(jnp.bfloat16), vw, preferred_element_type=jnp.float32)
            o = o / total
            lse = m + jnp.log2(total)
            for n, t in enumerate(tiles):
                part = o[:, n * LANES : (n + 1) * LANES].reshape(chunks, rows, LANES)
                start = head * size - t * LANES
                if start > 0:
                    old = osend[t, span].astype(jnp.float32)
                    part = jnp.where(lane1[None] >= start, part, old)
                osend[t, span] = part.astype(jnp.bfloat16)
            return lse

        lse = body(0, None)
        stat = sstat[...] if head else jnp.zeros((rows, LANES), jnp.float32)
        for j in range(NY):
            stat = jnp.where(lane1 == j * HEADS + head, lse[j * rows : (j + 1) * rows], stat)
        sstat[...] = stat
        return stat

    def o_move(t, d):
        dest = lax.rem(y + d, NY)
        return remote(osend.at[t, dest], orecv.at[t, d - 1], osem.at[t, d - 1], orsem.at[t, d - 1], at_y(dest))

    def s_move(d):
        dest = lax.rem(y + d, NY)
        return remote(ssend.at[dest], srecv.at[d - 1], ssem.at[d - 1], srsem.at[d - 1], at_y(dest))

    def head_and_send(head):
        stat = attend(head)
        for t in head_tiles(head, size):
            if (t * LANES + LANES - 1) // size == head:
                for d in range(1, NY):
                    o_move(t, d).start()
        if head == HEADS - 1:
            ssend[...] = stat.T[: NY * HEADS].reshape(NY, HEADS, rows)
            for d in range(1, NY):
                s_move(d).start()

    nstage = len(STAGES)
    steps = dict(own=own, near=near, far=far, here=here, head=head_and_send, w=w_step)
    w_first()
    for stage in range(AHEAD):
        own_q(stage)
        own(stage)
    for stage in range(AHEAD, nstage):
        own_q(stage)
    w_start()
    for line in ORDER:
        for word in line.split():
            steps[word[:-1]](int(word[-1]))

    w_step(4)
    for d in range(1, NY):
        s_move(d).wait_recv()

    lses = [ssend[y]] + [srecv[d - 1] for d in range(1, NY)]
    top = functools.reduce(jnp.maximum, lses)
    parts = [jnp.exp2(lse - top) for lse in lses]
    whole = functools.reduce(jnp.add, parts)
    weights = jnp.concatenate(
        [part / whole for part in parts] + [jnp.zeros((LANES - NY * HEADS, rows), jnp.float32)], axis=0
    ).T
    lane1 = lax.broadcasted_iota(jnp.int32, (1, LANES), 1)
    merged = []
    for t in range(ntile):
        first, last = t * LANES // size, (t * LANES + LANES - 1) // size
        cut = last * size - t * LANES
        total = None
        for j in range(NY):
            if j:
                o_move(t, j).wait_recv()
                value = orecv[t, j - 1]
            else:
                value = osend[t, y]
            a = weights[:, j * HEADS + first : j * HEADS + first + 1]
            b = weights[:, j * HEADS + last : j * HEADS + last + 1]
            term = jnp.where(lane1 < cut, a, b) * value.astype(jnp.float32)
            total = term if total is None else total + term
        merged.append(total.astype(jnp.bfloat16))
    attention = jnp.concatenate(merged, axis=1)

    w_shared(0, z).wait_recv()
    for step in range(1, nright + 1):
        w_shared(step, lax.rem(z + NZ - step, NZ)).wait_recv()
    for step in range(1, nleft + 1):
        w_shared(nright + step, lax.rem(z + step, NZ)).wait_recv()

    half = wbuf.shape[0] // 2
    ncols = half * wbuf.shape[1]
    for n in range(2):
        wn = wbuf[n * half : (n + 1) * half].reshape(ncols, ntile * LANES)
        out_ref[:, n * ncols : (n + 1) * ncols] = lax.dot_general(
            attention, wn, (((1,), (1,)), ((), ())), preferred_element_type=jnp.float32
        ).astype(jnp.bfloat16)

    for stage in range(nstage):
        for kind in range(2):
            q_move(stage, kind).wait_send()

        @pl.when(inner)
        def _():
            for kind in range(2, 4):
                q_move(stage, kind).wait_send()

        for i in range(len(kv_moves)):
            kv_send(stage, i).wait_send()
    for t in range(ntile):
        for d in range(1, NY):
            o_move(t, d).wait_send()
    for d in range(1, NY):
        s_move(d).wait_send()

    @pl.when(c == hi)
    def _():
        w_partner().wait_send()

    for step in range(1, nright + 1):
        w_ring(step, True, False).wait_send()
        w_share(step, z).wait_send()
    for step in range(1, nleft + 1):
        w_ring(step, False, False).wait_send()
        w_share(nright + step, z).wait_send()
    w_share(0, z).wait_send()


def per_device(queries, key_rows, value_rows, lengths, out_weight):
    rows, feats = queries.shape[1:]
    ntile = feats // LANES
    columns = out_weight.shape[1]
    nstage = len(STAGES)
    dma = pltpu.SemaphoreType.DMA
    anywhere = pl.BlockSpec(memory_space=pltpu.HBM)
    mixed = pl.pallas_call(
        kernel,
        out_shape=jax.ShapeDtypeStruct((rows, columns * 2 * NZ), jnp.bfloat16),
        in_specs=[pl.BlockSpec(memory_space=pltpu.SMEM)] + [anywhere] * 4,
        out_specs=pl.BlockSpec(memory_space=pltpu.VMEM),
        scratch_shapes=[
            pltpu.VMEM((ntile, NY, rows, LANES), jnp.bfloat16),
            pltpu.VMEM((2, ntile, NX * NC, rows, LANES), jnp.bfloat16),
            pltpu.VMEM((ntile, NY, rows, LANES), jnp.bfloat16),
            pltpu.VMEM((ntile, NY - 1, rows, LANES), jnp.bfloat16),
            pltpu.VMEM((rows, LANES), jnp.float32),
            pltpu.VMEM((NY, HEADS, rows), jnp.float32),
            pltpu.VMEM((NY - 1, HEADS, rows), jnp.float32),
            pltpu.VMEM((2 * NZ, columns, feats), jnp.bfloat16),
            dma((4, ntile)),
            dma((nstage, 9)),
            dma((nstage, 9)),
            dma((nstage, 4)),
            dma((nstage, 3)),
            dma((ntile, NY - 1)),
            dma((ntile, NY - 1)),
            dma((NY - 1,)),
            dma((NY - 1,)),
            dma((NZ // 2,)),
            dma((NZ // 2,)),
            dma((NZ // 2,)),
            dma((NZ // 2,)),
            dma((NZ,)),
            dma((NZ,)),
            dma((1,)),
            dma((1,)),
        ],
        compiler_params=pltpu.CompilerParams(
            collective_id=0, has_side_effects=True, vmem_limit_bytes=63 * 1024 * 1024
        ),
        name="attention",
    )(lengths, queries[0], key_rows[0], value_rows[0], out_weight.T)
    return mixed[None]


def solution(mesh):
    return jax.shard_map(
        per_device,
        mesh=mesh,
        in_specs=(
            P("fsdp", "ctx", None),
            P("fsdp", "ctx", None),
            P("fsdp", "ctx", None),
            P("fsdp"),
            P(None, "fsdp"),
        ),
        out_specs=P("fsdp", "ctx", None),
        check_vma=False,
    )
```
